128 devices in a mesh: leaf: 64 (over z, x, y), sub: 2 (over core).
Axes of the slice: x: 4, y: 4, z: 4, core: 2. Of those that a mesh axis runs over, the one named last changes fastest.
Arguments:
- right_sides: float32 [2, 4, 16, 6144], P(None, None, None, ('leaf', 'sub')), may hold values from -6 to 6
- diag_inverse: float32 [2, 6144, 11520], P(None, ('leaf', 'sub'))
- coupling: float32 [2, 6144, 5376], P(None, ('leaf', 'sub'))
- boundary: int32 [128, 5376], P(('leaf', 'sub')), may hold values from 0 to 10751, as said below
- plane_map: int32 [128, 192], P(('leaf', 'sub')), may hold values from 0 to 191, each once within a row
Outputs:
- plane_field: float32 [2, 16, 24576], P(None, None, ('leaf', 'sub'))
The draws below stay inside these ranges and needn't reach their ends.
Inputs may be any that keep to these rules, and one draw needn't show every extreme that they name: `boundary`: for level l >= 1 (columns e_l .. e_l + n_l - 1 of a row), entries lie in 0 .. (sum of n_a over a < l) - 1 and are equal on all devices d with the same d div (128 / 2^l); the first entry of each such segment is its largest allowed value and the second is 0.
All inputs are finite; a program needn't handle non-finite values.
Results may differ from the reference program's by a relative error of at most 0.0001.
Values sent between devices are 32-bit elements; how exact they have to be, the bound alone decides.
A program may use at most 64 MiB of HBM per device.

```python
import jax
import jax.numpy as jnp
from jax import lax

SEP_ROWS = 48
SOURCES = 16
LEVELS = 4
ROOT_ORDER = 6144
LOCAL_ROWS = 192
SLOTS = 3
N_LEAF = 64
N_SUB = 2
DEVICES = 128


def column_scales(first_level, factor):
    total_cols = sum((ROOT_ORDER // 2 ** level_index for level_index in range(first_level, LEVELS)))
    columns = jnp.arange(total_cols)
    scales = jnp.zeros((total_cols,), jnp.float32)
    offset = 0
    for level_index in range(first_level, LEVELS):
        front_order = ROOT_ORDER // 2 ** level_index
        inside = (columns >= offset) & (columns < offset + front_order)
        scales = jnp.where(inside, factor / jnp.sqrt(2.0 * front_order), scales)
        offset += front_order
    return (scales, total_cols)


def dense_draw(key, first_level, factor):
    scales, total_cols = column_scales(first_level, factor)
    values = jax.random.normal(key, (2, ROOT_ORDER, total_cols), jnp.float32)
    return values * scales[None, None, :]


def draw_diag_inverse(key, part):
    return dense_draw(jax.random.fold_in(key, 11), 0, 1.0)


def draw_coupling(key, part):
    return dense_draw(jax.random.fold_in(key, 23), 1, 0.6)


def draw_boundary(key, part):
    segments = []
    for level_index in range(1, LEVELS):
        nodes = 2 ** level_index
        front_order = ROOT_ORDER // nodes
        ancestry_len = sum((ROOT_ORDER // 2 ** upper for upper in range(level_index)))
        level_key = jax.random.fold_in(jax.random.fold_in(key, 37), level_index)
        indices = jax.random.randint(level_key, (nodes, front_order), 0, ancestry_len, jnp.int32)
        indices = indices.at[:, 0].set(ancestry_len - 1)
        indices = indices.at[:, 1].set(0)
        segments.append(jnp.repeat(indices, DEVICES // nodes, axis=0))
    return jnp.concatenate(segments, axis=1).astype(jnp.int32)


def block_levels(key, shape, cuts, smallest, high):
    level, own = 1.0, jax.random.fold_in(key, 6)
    for axis_at, blocks in cuts:
        steps = jnp.exp(jax.random.uniform(jax.random.fold_in(own, axis_at), (blocks,), jnp.float32, smallest / len(cuts), high / len(cuts)))
        level = level * jnp.repeat(steps, shape[axis_at] // blocks).reshape([-1 if axis == axis_at else 1 for axis in range(len(shape))])
    return level


def centred(key, dims, spread, limit, cuts=(), dtype=jnp.bfloat16):
    array = spread * jax.random.normal(key, dims, jnp.float32)
    if cuts:
        array = array * block_levels(key, dims, cuts, -0.22, 0.18)
    return jnp.clip(array, -limit, limit).astype(dtype)


def setup_inputs(seed: int = 0) -> dict:
    keys = jax.random.split(jax.random.key(seed), 6)
    return {
        "right_sides": centred(keys[0], (2, LEVELS, SOURCES, ROOT_ORDER), 1.0, 6.0, ((3, 128),), jnp.float32),
        "diag_inverse": draw_diag_inverse(jax.random.fold_in(keys[5], 71), 0),
        "coupling": draw_coupling(jax.random.fold_in(keys[5], 71), 0),
        "boundary": draw_boundary(jax.random.fold_in(keys[5], 71), 0),
        "plane_map": jax.vmap(lambda own: jax.random.permutation(own, LOCAL_ROWS))(jax.random.split(keys[4], DEVICES)).reshape((DEVICES, LOCAL_ROWS)).astype(jnp.int32),
    }


def complex_product(matrix, vectors):
    def mult(left, right):
        return jnp.einsum("sc,rc->sr", left, right, precision=lax.Precision.HIGHEST)
    real_part = mult(vectors[0], matrix[0]) - mult(vectors[1], matrix[1])
    imag_part = mult(vectors[0], matrix[1]) + mult(vectors[1], matrix[0])
    return jnp.stack([real_part, imag_part])


def reference(right_sides, diag_inverse, coupling, boundary, plane_map):
    devices_all = N_LEAF * N_SUB
    root_order = SEP_ROWS * devices_all
    solved = []
    diag_offset = 0
    couple_offset = 0
    for level_index in range(LEVELS):
        members = devices_all // 2 ** level_index
        front_order = SEP_ROWS * members
        pieces = []
        for node_index in range(2 ** level_index):
            first_row = node_index * front_order
            current = right_sides[:, level_index, :, first_row:first_row + front_order]
            if level_index > 0:
                parts = []
                for upper in range(level_index):
                    upper_order = root_order // 2 ** upper
                    upper_node = node_index >> (level_index - upper)
                    parts.append(solved[upper][:, :, upper_node * upper_order:(upper_node + 1) * upper_order])
                ancestry = jnp.concatenate(parts, axis=2)
                indices = boundary[node_index * members, couple_offset:couple_offset + front_order].astype(jnp.int32)
                gathered = jnp.take(ancestry, indices, axis=2)
                block = coupling[:, first_row:first_row + front_order, couple_offset:couple_offset + front_order]
                current = current - complex_product(block, gathered)
            block = diag_inverse[:, first_row:first_row + front_order, diag_offset:diag_offset + front_order]
            pieces.append(complex_product(block, current))
        solved.append(jnp.concatenate(pieces, axis=2))
        diag_offset += front_order
        if level_index > 0:
            couple_offset += front_order
    stacked = jnp.stack(solved, axis=1)
    stacked = stacked.reshape(2, LEVELS, SOURCES, devices_all, SEP_ROWS)
    local_rows = jnp.transpose(stacked, (3, 0, 2, 1, 4)).reshape(devices_all, 2, SOURCES, LOCAL_ROWS)
    picked = jnp.take_along_axis(local_rows, plane_map[:, None, None, :].astype(jnp.int32), axis=3)
    picked = picked.reshape(N_LEAF, N_SUB, 2, SOURCES, N_LEAF, SLOTS)
    picked = jnp.transpose(picked, (2, 3, 4, 1, 0, 5))
    return picked.reshape(2, SOURCES, devices_all * LOCAL_ROWS)
```

```python
import functools

import jax
import jax.numpy as jnp
from jax import lax
from jax.experimental import pallas as pl
from jax.experimental.pallas import tpu as pltpu
from jax.sharding import PartitionSpec as P

LEVELS = 4
GROUPS = 3
LANES = 128
MESH = pl.DeviceIdType.MESH
F32, BF16 = jnp.float32, jnp.bfloat16


def lane(rows):
    return lax.broadcasted_iota(jnp.int32, (rows, LANES), 1)


def roll(x, by):
    return pltpu.roll(x, by % LANES, 1)


def split(x):
    hi = x.astype(BF16)
    return hi, (x - hi.astype(F32)).astype(BF16)


def product(hi, lo, values):
    vhi, vlo = split(values)
    both = jnp.dot(hi, jnp.concatenate([vhi, vlo], axis=1), preferred_element_type=F32)
    rest = jnp.dot(lo, vhi, preferred_element_type=F32)
    return both[:, :LANES] + both[:, LANES:] + rest


def fold(t, rows, width):
    half = width // 2
    m = 2 * rows
    y = t[:m] + roll(t[m : 2 * m], -width) + roll(t[2 * m :], -2 * width)
    a, b = y[:rows], y[rows:]
    at = lane(rows)
    swapped = jnp.where(at < half, -roll(b, -half), roll(b, half))
    return a + swapped


def pack(x, part, width):
    at = lane(part)
    return jnp.where(
        at < width,
        x[:part],
        jnp.where(
            at < 2 * width, roll(x[part : 2 * part], width), roll(x[2 * part :], 2 * width)
        ),
    )


def repeat(x, at, group, width):
    v = jnp.where((at >= group * width) & (at < (group + 1) * width), x, 0.0)
    v = v + roll(v, width)
    return v + roll(v, 2 * width)


def body(
    chips, rows, orders, rs, d_hbm, u_hbm, bnd, pm, out, dv, uv, dp, up, perm, *rest
):
    bufs, (xu, bg, rt, sol, snd, rcv, load_sem, send_sem, recv_sem) = rest[:7], rest[7:]
    leaf, sub = lax.axis_index("leaf"), lax.axis_index("sub")
    part = rows // GROUPS
    width = rs.shape[0] * rs.shape[2]
    d_at = [sum(orders[:a]) for a in range(LEVELS + 1)]
    u_at = [0] + [sum(orders[1:a]) for a in range(1, LEVELS + 1)]

    loads = []
    for level in range(LEVELS):
        span = pl.ds(d_at[level], orders[level])
        loads.append(
            pltpu.make_async_copy(d_hbm.at[:, :, span], dv.at[:, :, span], load_sem.at[level])
        )
    loads.append(pltpu.make_async_copy(u_hbm, uv, load_sem.at[LEVELS]))
    for load in loads:
        load.start()

    def block(level):
        count = chips >> level
        return count, lax.rem(leaf, count), leaf - lax.rem(leaf, count)

    def send(stage, level, packed):
        buf = bufs[stage]
        count, mine, base = block(level)
        buf[sub, mine] = packed

        def one(k, carry):
            pltpu.make_async_remote_copy(
                src_ref=buf.at[sub, mine],
                dst_ref=buf.at[sub, mine],
                send_sem=send_sem.at[stage],
                recv_sem=recv_sem.at[stage],
                device_id=(base + lax.rem(mine + k, count), sub),
                device_id_type=MESH,
            ).start()
            return carry

        lax.fori_loop(1, count, one, 0)

    def forward(stage, level):
        buf = bufs[stage]
        count, _, _ = block(level)
        some = buf.at[sub, pl.ds(0, count - 1)]
        pltpu.make_async_copy(some, some, recv_sem.at[stage]).wait()
        copy = pltpu.make_async_remote_copy(
            src_ref=buf.at[sub],
            dst_ref=buf.at[sub],
            send_sem=send_sem.at[8 + stage],
            recv_sem=recv_sem.at[8 + stage],
            device_id=(leaf, 1 - sub),
            device_id_type=MESH,
        )
        copy.start()
        return copy

    def arrived(stage):
        other = bufs[stage].at[1 - sub]
        pltpu.make_async_copy(other, other, recv_sem.at[8 + stage]).wait()

    def prepare_diag(level):
        loads[level].wait()
        chunk = perm.shape[0]
        half = orders[level] // (2 * GROUPS)
        base = d_at[level] // GROUPS
        for t in range(orders[level] // chunk):
            at = d_at[level] + t * chunk
            hi, lo = split(dv[:, :, at : at + chunk].reshape(2 * rows, chunk))
            both = jnp.concatenate([hi, lo], axis=0)
            moved = jnp.dot(both, perm[...], preferred_element_type=F32).astype(BF16)
            for p in range(2):
                for g in range(GROUPS):
                    to = base + p * half + t * LANES
                    frm = (p * GROUPS + g) * LANES
                    for h in range(2):
                        dp[h, g, :, to : to + LANES] = moved[
                            h * 2 * rows : (h + 1) * 2 * rows, frm : frm + LANES
                        ]

    def prepare_coupling(level):
        k = orders[level] // GROUPS
        base = u_at[level] // GROUPS
        for g in range(GROUPS):
            at = u_at[level] + g * k
            hi, lo = split(uv[:, :, at : at + k].reshape(2 * rows, k))
            up[0, g, :, base : base + k] = hi
            up[1, g, :, base : base + k] = lo

    def diag_product(stage, level):
        buf = bufs[stage]
        half = orders[level] // (2 * GROUPS)
        base = d_at[level] // GROUPS
        copy = forward(stage, level)

        def part_of(p):
            at = pl.ds(pl.multiple_of(base + p * half, LANES), half)
            return product(
                dp[0, :, :, at].reshape(GROUPS * 2 * rows, half),
                dp[1, :, :, at].reshape(GROUPS * 2 * rows, half),
                buf[p].reshape(half, LANES),
            )

        total = part_of(sub)
        arrived(stage)
        total = total + part_of(1 - sub)
        copy.wait_send()
        return fold(total, rows, width)

    def collect(stage, level):
        buf = bufs[stage]
        count, _, _ = block(level)
        copy = forward(stage, level)
        at = lane(part)

        def spread(p):
            def one(c, carry):
                v = buf[p, c]
                for g in range(GROUPS):
                    to = d_at[level] + c * 2 * rows + p * rows + g * part
                    xu[pl.ds(pl.multiple_of(to, 16), part), :] = repeat(v, at, g, width)
                return carry

            lax.fori_loop(0, count, one, 0, unroll=4)

        spread(sub)
        arrived(stage)
        spread(1 - sub)
        copy.wait_send()

    def coupling_product(level):
        k = orders[level] // GROUPS
        at = lane(1)

        def one(i, carry):
            for u in range(8):
                j = i * 8 + u
                r = [
                    xu[pl.ds(bnd[0, u_at[level] + g * k + j], 1), :] for g in range(GROUPS)
                ]
                bg[pl.ds(j, 1), :] = jnp.where(
                    at < width, r[0], jnp.where(at < 2 * width, r[1], r[2])
                )
            return carry

        lax.fori_loop(0, k // 8, one, 0)
        base = u_at[level] // GROUPS
        return fold(
            product(
                up[0, :, :, base : base + k].reshape(GROUPS * 2 * rows, k),
                up[1, :, :, base : base + k].reshape(GROUPS * 2 * rows, k),
                bg[:k],
            ),
            rows,
            width,
        )

    def keep(level, x):
        sol[level * rows : (level + 1) * rows, :] = repeat(x, lane(rows), 0, width)

    for level in range(LEVELS):
        rt[level, :, :width] = jnp.transpose(rs[:, level].reshape(width, rows))
    send(0, 0, pack(rt[0], part, width))

    chunk = perm.shape[0]
    col = lax.broadcasted_iota(jnp.int32, (1, chunk), 1)
    block_at = jnp.right_shift(col, 7)
    second = (block_at >= GROUPS).astype(jnp.int32)
    source = (
        jnp.right_shift(col & 127, 4) * (2 * rows)
        + second * rows
        + (block_at - GROUPS * second) * part
        + (col & 15)
    )
    row = lax.broadcasted_iota(jnp.int32, (chunk, chunk), 0)
    perm[...] = jnp.where(row == source, 1.0, 0.0).astype(BF16)

    prepare_diag(0)
    x = diag_product(0, 0)
    keep(0, x)
    send(1, 0, pack(x, part, width))
    loads[LEVELS].wait()
    for level in range(1, LEVELS):
        prepare_coupling(level)
        prepare_diag(level)
    for level in range(1, LEVELS):
        collect(2 * level - 1, level - 1)
        z = rt[level] - coupling_product(level)
        send(2 * level, level, pack(z, part, width))
        x = diag_product(2 * level, level)
        keep(level, x)
        if level + 1 < LEVELS:
            send(2 * level + 1, level, pack(x, part, width))

    at = lane(1)

    def pick(j, carry):
        r = [sol[pl.ds(pm[0, GROUPS * j + p], 1), :] for p in range(GROUPS)]
        snd[j] = jnp.where(at < width, r[0], jnp.where(at < 2 * width, r[1], r[2]))
        return carry

    lax.fori_loop(0, chips, pick, 0, unroll=8)
    rcv[leaf] = snd[leaf]

    def one(k, carry):
        to = lax.rem(leaf + k, chips)
        pltpu.make_async_remote_copy(
            src_ref=snd.at[to],
            dst_ref=rcv.at[leaf],
            send_sem=send_sem.at[7],
            recv_sem=recv_sem.at[7],
            device_id=(to, sub),
            device_id_type=MESH,
        ).start()
        return carry

    lax.fori_loop(1, chips, one, 0)
    some = rcv.at[pl.ds(0, chips - 1)]
    pltpu.make_async_copy(some, some, recv_sem.at[7]).wait()
    got = rcv[...].reshape(chips, LANES)
    frm = lax.broadcasted_iota(jnp.int32, (chips, GROUPS * chips), 0)
    to = lax.broadcasted_iota(jnp.int32, (chips, GROUPS * chips), 1)
    total = jnp.zeros((width, GROUPS * chips), F32)
    for p in range(GROUPS):
        place = jnp.where(frm * GROUPS + p == to, 1.0, 0.0)
        moved = lax.dot_general(
            got, place, (((0,), (0,)), ((), ())),
            precision=lax.Precision.HIGHEST, preferred_element_type=F32,
        )
        total = total + moved[p * width : (p + 1) * width]
    out[...] = total

    for stage in range(7):
        count = chips >> ((stage + 1) // 2 if stage % 2 == 0 else stage // 2)
        some = bufs[stage].at[sub, pl.ds(0, count - 1)]
        pltpu.make_async_copy(some, some, send_sem.at[stage]).wait()
    some = snd.at[pl.ds(0, chips - 1)]
    pltpu.make_async_copy(some, some, send_sem.at[7]).wait()


def local(right_sides, diag_inverse, coupling, boundary, plane_map):
    chips = lax.axis_size("leaf")
    rows = right_sides.shape[3]
    part = rows // GROUPS
    width = right_sides.shape[0] * right_sides.shape[2]
    orders = [2 * chips * rows >> level for level in range(LEVELS)]
    d_cols, u_cols = sum(orders), sum(orders[1:])
    chunk = 2 * GROUPS * LANES
    stage_levels = [0, 0, 1, 1, 2, 2, 3]
    scratch = [
        pltpu.VMEM((2, rows, d_cols), F32),
        pltpu.VMEM((2, rows, u_cols), F32),
        pltpu.VMEM((2, GROUPS, 2 * rows, d_cols // GROUPS), BF16),
        pltpu.VMEM((2, GROUPS, 2 * rows, u_cols // GROUPS), BF16),
        pltpu.VMEM((chunk, chunk), BF16),
        *[pltpu.VMEM((2, chips >> level, part, LANES), F32) for level in stage_levels],
        pltpu.VMEM((sum(orders[:-1]), LANES), F32),
        pltpu.VMEM((orders[1] // GROUPS, LANES), F32),
        pltpu.VMEM((LEVELS, rows, LANES), F32),
        pltpu.VMEM((LEVELS * rows, LANES), F32),
        pltpu.VMEM((chips, 1, LANES), F32),
        pltpu.VMEM((chips, 1, LANES), F32),
        pltpu.SemaphoreType.DMA((LEVELS + 1,)),
        pltpu.SemaphoreType.DMA((16,)),
        pltpu.SemaphoreType.DMA((16,)),
    ]
    vmem, smem, whole = (
        pl.BlockSpec(memory_space=s) for s in (pltpu.VMEM, pltpu.SMEM, pl.ANY)
    )
    field = pl.pallas_call(
        functools.partial(body, chips, rows, orders),
        out_shape=jax.ShapeDtypeStruct((width, GROUPS * chips), F32),
        in_specs=[vmem, whole, whole, smem, smem],
        out_specs=vmem,
        scratch_shapes=scratch,
        compiler_params=pltpu.CompilerParams(
            has_side_effects=True, vmem_limit_bytes=44 << 20
        ),
    )(right_sides, diag_inverse, coupling, boundary, plane_map)
    return field.reshape(2, width // 2, GROUPS * chips)


def solution(mesh):
    in_specs = (
        P(None, None, None, ("leaf", "sub")),
        P(None, ("leaf", "sub"), None),
        P(None, ("leaf", "sub"), None),
        P(("leaf", "sub"), None),
        P(("leaf", "sub"), None),
    )
    out_specs = P(None, None, ("leaf", "sub"))
    return jax.shard_map(local, mesh=mesh, in_specs=in_specs, out_specs=out_specs, check_vma=False)
```

```python
import functools

import jax
import jax.numpy as jnp
from jax import lax
from jax.experimental import pallas as pl
from jax.experimental.pallas import tpu as pltpu
from jax.sharding import PartitionSpec as P

LEVELS = 4
GROUPS = 3
LANES = 128
TILE = 256
SPAN = 4096
DIRECT = 2
CUTS = (0.35, 0.6)
MESH = pl.DeviceIdType.MESH
F32, BF16 = jnp.float32, jnp.bfloat16


def lane(rows):
    return lax.broadcasted_iota(jnp.int32, (rows, LANES), 1)


def roll(x, by):
    return pltpu.roll(x, by % LANES, 1)


def split(x):
    hi = x.astype(BF16)
    return hi, (x - hi.astype(F32)).astype(BF16)


def product(hi, lo, values):
    both = jnp.dot(hi, values, preferred_element_type=F32)
    rest = jnp.dot(lo, values[:, :LANES], preferred_element_type=F32)
    return both[:, :LANES] + both[:, LANES:] + rest


def fold(t, rows, width):
    half = width // 2
    m = 2 * rows
    y = t[:m] + roll(t[m : 2 * m], -width) + roll(t[2 * m :], -2 * width)
    a, b = y[:rows], y[rows:]
    at = lane(rows)
    swapped = jnp.where(at < half, -roll(b, -half), roll(b, half))
    return a + swapped


def pack(x, part, width):
    at = lane(part)
    return jnp.where(
        at < width,
        x[:part],
        jnp.where(
            at < 2 * width, roll(x[part : 2 * part], width), roll(x[2 * part :], 2 * width)
        ),
    )


def repeat(x, width):
    v = jnp.where(lane(x.shape[0]) < width, x, 0.0)
    v = v + roll(v, width)
    return v + roll(v, 2 * width)


def offsets(count):
    sizes = (max(count // 16, 1), min(max(count // 4, 1), 4), min(count, 4))
    steps = [
        (a, b, c)
        for a in range(sizes[0])
        for b in range(sizes[1])
        for c in range(sizes[2])
        if a or b or c
    ]
    hops = lambda step: sum(min(s, n - s) for s, n in zip(step, sizes))
    return sizes, sorted(steps, key=lambda step: -hops(step))


def body(
    chips, rows, orders, rs_hbm, d_hbm, u_hbm, bnd_hbm, pm_hbm, out, *rest
):
    (rs, bnd, pm, dv, uv, dp, uc, perm, qb, xb, ahead), rest = rest[:11], rest[11:]
    ups, bufs, rest = (None,) + rest[:3], rest[3:10], rest[10:]
    rt, sol, snd, rcv, load_sem, send_sem, recv_sem = rest
    leaf, sub = lax.axis_index("leaf"), lax.axis_index("sub")
    part = rows // GROUPS
    width = rs_hbm.shape[0] * rs_hbm.shape[2]
    tall = GROUPS * 2 * rows
    d_at = [sum(orders[:a]) for a in range(LEVELS + 1)]
    u_at = [0] + [sum(orders[1:a]) for a in range(1, LEVELS + 1)]
    k_at = [a // GROUPS for a in d_at]
    halves = [n // (2 * GROUPS) for n in orders]

    barrier = pltpu.get_barrier_semaphore()

    def chip(step, sizes, count):
        mine = lax.rem(leaf, count)
        z, x, y = mine // 16, lax.rem(mine // 4, 4), lax.rem(mine, 4)
        to = [lax.rem(at + s, n) for at, s, n in zip((z, x, y), step, sizes)]
        return leaf - mine + to[0] * 16 + to[1] * 4 + to[2]

    sizes, steps = offsets(chips)
    for step in steps:
        pl.semaphore_signal(
            barrier, inc=1, device_id=(chip(step, sizes, chips), sub), device_id_type=MESH
        )
    pl.semaphore_signal(barrier, inc=1, device_id=(leaf, 1 - sub), device_id_type=MESH)

    first = pltpu.make_async_copy(rs_hbm, rs, load_sem.at[LEVELS + 1])
    first.start()
    loads = []
    for level in range(LEVELS):
        span = pl.ds(d_at[level], orders[level])
        loads.append(
            pltpu.make_async_copy(d_hbm.at[:, :, span], dv.at[:, :, span], load_sem.at[level])
        )
    loads.append(pltpu.make_async_copy(u_hbm, uv, load_sem.at[LEVELS]))
    for i in range(bnd.shape[0]):
        pltpu.make_async_copy(
            bnd_hbm.at[:, pl.ds(i * LANES, LANES)], bnd.at[i], load_sem.at[LEVELS + 2]
        ).start()
    loads.append(pltpu.make_async_copy(bnd, bnd, load_sem.at[LEVELS + 2]))
    loads.append(pltpu.make_async_copy(pm_hbm, pm, load_sem.at[LEVELS + 3]))
    for load in (loads[LEVELS], *loads[:LEVELS], loads[-1]):
        load.start()

    def block(level):
        count = chips >> level
        return count, lax.rem(leaf, count)

    def send(stage, level, packed):
        buf = bufs[stage]
        count, mine = block(level)
        buf[sub, mine] = packed
        sizes, steps = offsets(count)

        def copy(to, core, sem):
            pltpu.make_async_remote_copy(
                src_ref=buf.at[sub, mine],
                dst_ref=buf.at[sub, mine],
                send_sem=send_sem.at[sem],
                recv_sem=recv_sem.at[sem],
                device_id=(to, core),
                device_id_type=MESH,
            ).start()

        for step in steps:
            to = chip(step, sizes, count)
            copy(to, sub, stage)
            if level >= DIRECT:
                copy(to, 1 - sub, 8 + stage)
        if level >= DIRECT:
            copy(leaf, 1 - sub, 8 + stage)

    def near(stage, level):
        buf = bufs[stage]
        count, _ = block(level)
        some = buf.at[sub, pl.ds(0, count - 1)]
        pltpu.make_async_copy(some, some, recv_sem.at[stage]).wait()
        if level < DIRECT:
            pltpu.make_async_remote_copy(
                src_ref=buf.at[sub],
                dst_ref=buf.at[sub],
                send_sem=send_sem.at[8 + stage],
                recv_sem=recv_sem.at[8 + stage],
                device_id=(leaf, 1 - sub),
                device_id_type=MESH,
            ).start()

    def far(stage, level):
        other = bufs[stage].at[1 - sub]
        pltpu.make_async_copy(other, other, recv_sem.at[8 + stage]).wait()

    def values(stage, level, p):
        return jnp.concatenate(split(bufs[stage][p].reshape(halves[level], LANES)), axis=1)

    def prepare_diag(level):
        loads[level].wait()
        chunk = perm.shape[0]
        for t in range(orders[level] // chunk):
            at = d_at[level] + t * chunk
            hi, lo = split(dv[:, :, at : at + chunk].reshape(2 * rows, chunk))
            both = jnp.concatenate([hi, lo], axis=0)
            moved = jnp.dot(both, perm[...], preferred_element_type=F32).astype(BF16)
            for p in range(2):
                for g in range(GROUPS):
                    to = k_at[level] + p * halves[level] + t * LANES
                    frm = (p * GROUPS + g) * LANES
                    for h in range(2):
                        dp[h, g, :, to : to + LANES] = moved[
                            h * 2 * rows : (h + 1) * 2 * rows, frm : frm + LANES
                        ]

    def both_halves(stage, level, part_of):
        near(stage, level)
        total = part_of(sub)
        far(stage, level)
        return total + part_of(1 - sub)

    def diag_product(stage, level):
        def part_of(p):
            at = pl.ds(pl.multiple_of(k_at[level] + p * halves[level], LANES), halves[level])
            return product(
                dp[0, :, :, at].reshape(tall, halves[level]),
                dp[1, :, :, at].reshape(tall, halves[level]),
                values(stage, level, p),
            )

        return fold(both_halves(stage, level, part_of), rows, width)

    def coupled(level, at, size):
        return product(
            ups[level][0, :, :, pl.ds(at, size)].reshape(tall, size),
            ups[level][1, :, :, pl.ds(at, size)].reshape(tall, size),
            xb[pl.ds(at, size), :],
        )

    def coupling_product(stage, level):
        up = level - 1

        def part_of(p):
            at = pl.multiple_of(k_at[up] + p * halves[up], LANES)
            xb[pl.ds(at, halves[up]), :] = values(stage, up, p)
            return coupled(level, at, halves[up])

        total = both_halves(stage, up, part_of)
        if level > 1:
            total = total + ahead[...]
        return fold(total, rows, width)

    def multiply_ahead(level):
        total = coupled(level, 0, k_at[1])
        for up in range(1, level - 1):
            total = total + coupled(level, k_at[up], k_at[up + 1] - k_at[up])
        ahead[...] = total

    def place_boundary():
        loads[LEVELS + 1].wait()
        index = bnd[...].reshape(bnd.shape[0], LANES)
        at, base, half = index, jnp.zeros_like(index), jnp.full_like(index, halves[0])
        for up in range(1, LEVELS - 1):
            below = index >= d_at[up]
            at = jnp.where(below, index - d_at[up], at)
            base = jnp.where(below, k_at[up], base)
            half = jnp.where(below, halves[up], half)
        owner = jnp.right_shift(at * ((1 << 21) // rows + 1), 21)
        inside = at - owner * rows
        group = jnp.right_shift(inside, 4)
        packed = base + (owner & 1) * half + jnp.right_shift(owner, 1) * part + (inside & 15)
        packed = jnp.transpose(group * SPAN + packed)
        for i in range(bnd.shape[0]):
            qb[i * LANES : (i + 1) * LANES, :] = jnp.broadcast_to(
                packed[:, i : i + 1], (LANES, LANES)
            )

    def split_coupling():
        loads[LEVELS].wait()
        for level in range(1, LEVELS):
            at = slice(u_at[level], u_at[level + 1])
            hi, lo = split(uv[:, :, at].reshape(2 * rows, orders[level]))
            uc[: 2 * rows, at] = hi
            uc[2 * rows :, at] = lo

    def select(level, begin, end):
        span = slice(u_at[level], u_at[level + 1])
        tiles = k_at[level] // TILE

        def one(t, carry):
            g = t // tiles
            k = pl.multiple_of((t - g * tiles) * TILE, TILE)
            want = lane(1) + (g * SPAN + k)
            q = qb[span, :]
            picks = [
                jnp.where(q == want + i * LANES, 1.0, 0.0).astype(BF16)
                for i in range(TILE // LANES)
            ]
            moved = jnp.dot(
                uc[:, span], jnp.concatenate(picks, axis=1), preferred_element_type=F32
            )
            hi, lo = split(moved[: 2 * rows] + moved[2 * rows :])
            ups[level][0, g, :, pl.ds(k, TILE)] = hi
            ups[level][1, g, :, pl.ds(k, TILE)] = lo
            return carry

        count = GROUPS * tiles
        lax.fori_loop(int(count * begin), int(count * end), one, 0)

    def keep(level, x):
        sol[level * rows : (level + 1) * rows, :] = repeat(x, width)

    first.wait()
    for level in range(LEVELS):
        rt[level, :, :width] = jnp.transpose(rs[:, level].reshape(width, rows))
    place_boundary()
    split_coupling()
    select(1, 0, CUTS[0])
    pl.semaphore_wait(barrier, chips)
    send(0, 0, pack(rt[0], part, width))

    chunk = perm.shape[0]
    col = lax.broadcasted_iota(jnp.int32, (1, chunk), 1)
    block_at = jnp.right_shift(col, 7)
    second = (block_at >= GROUPS).astype(jnp.int32)
    source = (
        jnp.right_shift(col & 127, 4) * (2 * rows)
        + second * rows
        + (block_at - GROUPS * second) * part
        + (col & 15)
    )
    row = lax.broadcasted_iota(jnp.int32, (chunk, chunk), 0)
    perm[...] = jnp.where(row == source, 1.0, 0.0).astype(BF16)
    prepare_diag(0)
    select(1, CUTS[0], CUTS[1])
    x = diag_product(0, 0)
    keep(0, x)
    send(1, 0, pack(x, part, width))
    select(1, CUTS[1], 1)
    prepare_diag(1)
    for level in range(1, LEVELS):
        z = rt[level] - coupling_product(2 * level - 1, level)
        send(2 * level, level, pack(z, part, width))
        if level + 1 < LEVELS:
            prepare_diag(level + 1)
            select(level + 1, 0, 0.5)
        x = diag_product(2 * level, level)
        keep(level, x)
        if level + 1 < LEVELS:
            send(2 * level + 1, level, pack(x, part, width))
            select(level + 1, 0.5, 1)
            multiply_ahead(level + 1)

    loads[-1].wait()
    at = lane(1)

    def pick(j, carry):
        r = [sol[pl.ds(pm[0, GROUPS * j + p], 1), :] for p in range(GROUPS)]
        snd[j] = jnp.where(at < width, r[0], jnp.where(at < 2 * width, r[1], r[2]))
        return carry

    lax.fori_loop(0, chips, pick, 0, unroll=8)
    rcv[leaf] = snd[leaf]
    sizes, steps = offsets(chips)
    for step in steps:
        to = chip(step, sizes, chips)
        pltpu.make_async_remote_copy(
            src_ref=snd.at[to],
            dst_ref=rcv.at[leaf],
            send_sem=send_sem.at[7],
            recv_sem=recv_sem.at[7],
            device_id=(to, sub),
            device_id_type=MESH,
        ).start()
    some = rcv.at[pl.ds(0, chips - 1)]
    pltpu.make_async_copy(some, some, recv_sem.at[7]).wait()
    got = rcv[...].reshape(chips, LANES)
    frm = lax.broadcasted_iota(jnp.int32, (chips, GROUPS * chips), 0)
    to = lax.broadcasted_iota(jnp.int32, (chips, GROUPS * chips), 1)
    total = jnp.zeros((width, GROUPS * chips), F32)
    for p in range(GROUPS):
        place = jnp.where(frm * GROUPS + p == to, 1.0, 0.0)
        moved = lax.dot_general(
            got, place, (((0,), (0,)), ((), ())),
            precision=lax.Precision.HIGHEST, preferred_element_type=F32,
        )
        total = total + moved[p * width : (p + 1) * width]
    out[...] = total

    for stage in range(7):
        level = (stage + 1) // 2 if stage % 2 == 0 else stage // 2
        some = bufs[stage].at[sub, pl.ds(0, (chips >> level) - 1)]
        pltpu.make_async_copy(some, some, send_sem.at[stage]).wait()
        some = bufs[stage].at[sub]
        pltpu.make_async_copy(some, some, send_sem.at[8 + stage]).wait()
    some = snd.at[pl.ds(0, chips - 1)]
    pltpu.make_async_copy(some, some, send_sem.at[7]).wait()


def local(right_sides, diag_inverse, coupling, boundary, plane_map):
    chips = lax.axis_size("leaf")
    rows = right_sides.shape[3]
    part = rows // GROUPS
    width = right_sides.shape[0] * right_sides.shape[2]
    orders = [2 * chips * rows >> level for level in range(LEVELS)]
    d_cols, u_cols = sum(orders), sum(orders[1:])
    chunk = 2 * GROUPS * LANES
    stage_levels = [0, 0, 1, 1, 2, 2, 3]
    packed = [sum(orders[:level]) // GROUPS for level in range(LEVELS)]
    scratch = [
        pltpu.VMEM(right_sides.shape, F32),
        pltpu.VMEM((u_cols // LANES, 1, LANES), jnp.int32),
        pltpu.SMEM(plane_map.shape, jnp.int32),
        pltpu.VMEM((2, rows, d_cols), F32),
        pltpu.VMEM((2, rows, u_cols), F32),
        pltpu.VMEM((2, GROUPS, 2 * rows, d_cols // GROUPS), BF16),
        pltpu.VMEM((4 * rows, u_cols), BF16),
        pltpu.VMEM((chunk, chunk), BF16),
        pltpu.VMEM((u_cols, LANES), jnp.int32),
        pltpu.VMEM((packed[-1], 2 * LANES), BF16),
        pltpu.VMEM((GROUPS * 2 * rows, LANES), F32),
        *[pltpu.VMEM((2, GROUPS, 2 * rows, k), BF16) for k in packed[1:]],
        *[pltpu.VMEM((2, chips >> level, part, LANES), F32) for level in stage_levels],
        pltpu.VMEM((LEVELS, rows, LANES), F32),
        pltpu.VMEM((LEVELS * rows, LANES), F32),
        pltpu.VMEM((chips, 1, LANES), F32),
        pltpu.VMEM((chips, 1, LANES), F32),
        pltpu.SemaphoreType.DMA((LEVELS + 4,)),
        pltpu.SemaphoreType.DMA((16,)),
        pltpu.SemaphoreType.DMA((16,)),
    ]
    vmem, hbm = (pl.BlockSpec(memory_space=s) for s in (pltpu.VMEM, pltpu.HBM))
    field = pl.pallas_call(
        functools.partial(body, chips, rows, orders),
        out_shape=jax.ShapeDtypeStruct((width, GROUPS * chips), F32),
        in_specs=[hbm] * 5,
        out_specs=vmem,
        scratch_shapes=scratch,
        compiler_params=pltpu.CompilerParams(
            collective_id=0, has_side_effects=True, vmem_limit_bytes=60 << 20
        ),
    )(right_sides, diag_inverse, coupling, boundary, plane_map)
    return field.reshape(2, width // 2, GROUPS * chips)


def solution(mesh):
    in_specs = (
        P(None, None, None, ("leaf", "sub")),
        P(None, ("leaf", "sub"), None),
        P(None, ("leaf", "sub"), None),
        P(("leaf", "sub"), None),
        P(("leaf", "sub"), None),
    )
    out_specs = P(None, None, ("leaf", "sub"))
    return jax.shard_map(local, mesh=mesh, in_specs=in_specs, out_specs=out_specs, check_vma=False)
```

```python
import functools

import jax
import jax.numpy as jnp
from jax import lax
from jax.experimental import pallas as pl
from jax.experimental.pallas import tpu as pltpu
from jax.sharding import PartitionSpec as P

LEVELS = 4
SENT = 12
GROUPS = 3
LANES = 128
TILE = 512
SPAN = 4096
DIRECT = 2
PLAN = (
    (),
    ((1, 0, 3),),
    ((1, 3, 12),),
    ((2, 0, 9),),
    ((2, 9, 18),),
    ((3, 0, 9),),
    ((3, 9, 21),),
)
MESH = pl.DeviceIdType.MESH
F32, BF16 = jnp.float32, jnp.bfloat16


def lane(rows):
    return lax.broadcasted_iota(jnp.int32, (rows, LANES), 1)


def roll(x, by):
    return pltpu.roll(x, by % LANES, 1)


def split(x):
    hi = x.astype(BF16)
    return hi, (x - hi.astype(F32)).astype(BF16)


def product(hi, lo, values):
    both = jnp.dot(hi, values, preferred_element_type=F32)
    rest = jnp.dot(lo, values[:, :LANES], preferred_element_type=F32)
    return both[:, :LANES] + both[:, LANES:] + rest


def fold(t, rows, width):
    half = width // 2
    m = 2 * rows
    y = t[:m] + roll(t[m : 2 * m], -width) + roll(t[2 * m :], -2 * width)
    a, b = y[:rows], y[rows:]
    at = lane(rows)
    swapped = jnp.where(at < half, -roll(b, -half), roll(b, half))
    return a + swapped


def pack(x, part, width):
    at = lane(part)
    return jnp.where(
        at < width,
        x[:part],
        jnp.where(
            at < 2 * width, roll(x[part : 2 * part], width), roll(x[2 * part :], 2 * width)
        ),
    )


def squeeze(block, x, part, width):
    last = [x[g * part + 8 : g * part + 16] for g in range(GROUPS)]
    sub8 = lax.broadcasted_iota(jnp.int32, (8, LANES), 0)
    spare = jnp.where(sub8 < 4, pltpu.roll(last[0], 4, 0), last[1])
    free = lane(8) < GROUPS * width
    top = jnp.where(free, block[:8], roll(spare, GROUPS * width))
    low = jnp.where(free, block[8:], roll(pltpu.roll(last[2], 4, 0), GROUPS * width))
    return top, low


def restore(top, low, width):
    at = lax.broadcasted_iota(jnp.int32, top.shape, 2)
    sub8 = lax.broadcasted_iota(jnp.int32, top.shape, 1)
    turn = lambda v, by: pltpu.roll(v, by % LANES, 2)
    outer = jnp.where(at < width, turn(top, width), turn(low, 3 * width))
    outer = pltpu.roll(outer, 4, 1)
    inner = (at >= width) & (at < 2 * width)
    moved = jnp.where(inner, turn(top, 2 * width), outer)
    low = jnp.where(sub8 < 4, low, moved)
    return jnp.concatenate([top, low], axis=1).reshape(-1, LANES)


def repeat(x, width):
    v = jnp.where(lane(x.shape[0]) < width, x, 0.0)
    v = v + roll(v, width)
    return v + roll(v, 2 * width)


def offsets(count):
    sizes = (max(count // 16, 1), min(max(count // 4, 1), 4), min(count, 4))
    steps = [
        (a, b, c)
        for a in range(sizes[0])
        for b in range(sizes[1])
        for c in range(sizes[2])
        if a or b or c
    ]
    hops = lambda step: sum(min(s, n - s) for s, n in zip(step, sizes))
    return sizes, sorted(steps, key=lambda step: -hops(step))


def body(
    chips, rows, orders, rs_hbm, d_hbm, u_hbm, bnd_hbm, pm_hbm, out, *rest
):
    (rs, bnd, pm, dv, uv, dp, uc, perm, qb, xb, ahead), rest = rest[:11], rest[11:]
    ups, bufs, rest = (None,) + rest[:3], rest[3:10], rest[10:]
    rt, sol, snd, rcv, load_sem, send_sem, recv_sem = rest
    leaf, sub = lax.axis_index("leaf"), lax.axis_index("sub")
    part = rows // GROUPS
    width = rs_hbm.shape[0] * rs_hbm.shape[2]
    tall = GROUPS * 2 * rows
    d_at = [sum(orders[:a]) for a in range(LEVELS + 1)]
    u_at = [0] + [sum(orders[1:a]) for a in range(1, LEVELS + 1)]
    k_at = [a // GROUPS for a in d_at]
    halves = [n // (2 * GROUPS) for n in orders]

    barrier = pltpu.get_barrier_semaphore()

    def chip(step, sizes, count):
        mine = lax.rem(leaf, count)
        z, x, y = mine // 16, lax.rem(mine // 4, 4), lax.rem(mine, 4)
        to = [lax.rem(at + s, n) for at, s, n in zip((z, x, y), step, sizes)]
        return leaf - mine + to[0] * 16 + to[1] * 4 + to[2]

    sizes, steps = offsets(chips)
    for step in steps:
        pl.semaphore_signal(
            barrier, inc=1, device_id=(chip(step, sizes, chips), sub), device_id_type=MESH
        )
    pl.semaphore_signal(barrier, inc=1, device_id=(leaf, 1 - sub), device_id_type=MESH)

    first = pltpu.make_async_copy(rs_hbm, rs, load_sem.at[LEVELS + 1])
    first.start()
    loads = []
    for level in range(LEVELS):
        span = pl.ds(d_at[level], orders[level])
        loads.append(
            pltpu.make_async_copy(d_hbm.at[:, :, span], dv.at[:, :, span], load_sem.at[level])
        )
    loads.append(pltpu.make_async_copy(u_hbm, uv, load_sem.at[LEVELS]))
    for i in range(bnd.shape[0]):
        pltpu.make_async_copy(
            bnd_hbm.at[:, pl.ds(i * LANES, LANES)], bnd.at[i], load_sem.at[LEVELS + 2]
        ).start()
    loads.append(pltpu.make_async_copy(bnd, bnd, load_sem.at[LEVELS + 2]))
    loads.append(pltpu.make_async_copy(pm_hbm, pm, load_sem.at[LEVELS + 3]))
    for load in (loads[LEVELS], *loads[:LEVELS], loads[-1]):
        load.start()

    def block(level):
        count = chips >> level
        return count, lax.rem(leaf, count)

    def send(stage, level, x):
        buf = bufs[stage]
        count, mine = block(level)
        top, low = squeeze(pack(x, part, width), x, part, width)
        buf[sub, mine, :8] = top
        buf[sub, mine, 8:] = low
        sizes, steps = offsets(count)

        def copy(to, core, sem):
            pltpu.make_async_remote_copy(
                src_ref=buf.at[sub, mine, pl.ds(0, SENT)],
                dst_ref=buf.at[sub, mine, pl.ds(0, SENT)],
                send_sem=send_sem.at[sem],
                recv_sem=recv_sem.at[sem],
                device_id=(to, core),
                device_id_type=MESH,
            ).start()

        for step in steps:
            to = chip(step, sizes, count)
            copy(to, sub, stage)
            if level >= DIRECT:
                copy(to, 1 - sub, 8 + stage)
        if level >= DIRECT:
            copy(leaf, 1 - sub, 8 + stage)

    def near(stage, level):
        buf = bufs[stage]
        count, _ = block(level)
        some = buf.at[sub, pl.ds(0, count - 1), pl.ds(0, SENT)]
        pltpu.make_async_copy(some, some, recv_sem.at[stage]).wait()
        if level < DIRECT:
            pltpu.make_async_remote_copy(
                src_ref=buf.at[sub, :, pl.ds(0, SENT)],
                dst_ref=buf.at[sub, :, pl.ds(0, SENT)],
                send_sem=send_sem.at[8 + stage],
                recv_sem=recv_sem.at[8 + stage],
                device_id=(leaf, 1 - sub),
                device_id_type=MESH,
            ).start()

    def far(stage, level):
        other = bufs[stage].at[1 - sub, :, pl.ds(0, SENT)]
        pltpu.make_async_copy(other, other, recv_sem.at[8 + stage]).wait()

    def values(stage, level, p):
        buf = bufs[stage]
        rows_of = restore(buf[p, :, :8], buf[p, :, 8:], width)
        return jnp.concatenate(split(rows_of), axis=1)

    def prepare_diag(level):
        loads[level].wait()
        chunk = perm.shape[0]
        for t in range(orders[level] // chunk):
            at = d_at[level] + t * chunk
            hi, lo = split(dv[:, :, at : at + chunk].reshape(2 * rows, chunk))
            both = jnp.concatenate([hi, lo], axis=0)
            moved = jnp.dot(both, perm[...], preferred_element_type=F32).astype(BF16)
            for p in range(2):
                for g in range(GROUPS):
                    to = k_at[level] + p * halves[level] + t * LANES
                    frm = (p * GROUPS + g) * LANES
                    for h in range(2):
                        dp[h, g, :, to : to + LANES] = moved[
                            h * 2 * rows : (h + 1) * 2 * rows, frm : frm + LANES
                        ]

    def both_halves(stage, level, part_of):
        near(stage, level)
        total = part_of(sub)
        far(stage, level)
        return total + part_of(1 - sub)

    def diag_product(stage, level):
        def part_of(p):
            at = pl.ds(pl.multiple_of(k_at[level] + p * halves[level], LANES), halves[level])
            return product(
                dp[0, :, :, at].reshape(tall, halves[level]),
                dp[1, :, :, at].reshape(tall, halves[level]),
                values(stage, level, p),
            )

        return fold(both_halves(stage, level, part_of), rows, width)

    def coupled(level, at, size):
        return product(
            ups[level][0, :, :, pl.ds(at, size)].reshape(tall, size),
            ups[level][1, :, :, pl.ds(at, size)].reshape(tall, size),
            xb[pl.ds(at, size), :],
        )

    def coupling_product(stage, level):
        up = level - 1

        def part_of(p):
            at = pl.multiple_of(k_at[up] + p * halves[up], LANES)
            xb[pl.ds(at, halves[up]), :] = values(stage, up, p)
            return coupled(level, at, halves[up])

        total = both_halves(stage, up, part_of)
        if level > 1:
            total = total + ahead[...]
        return fold(total, rows, width)

    def multiply_ahead(level):
        total = coupled(level, 0, k_at[1])
        for up in range(1, level - 1):
            total = total + coupled(level, k_at[up], k_at[up + 1] - k_at[up])
        ahead[...] = total

    def place_boundary():
        loads[LEVELS + 1].wait()
        index = bnd[...].reshape(bnd.shape[0], LANES)
        at, base, half = index, jnp.zeros_like(index), jnp.full_like(index, halves[0])
        for up in range(1, LEVELS - 1):
            below = index >= d_at[up]
            at = jnp.where(below, index - d_at[up], at)
            base = jnp.where(below, k_at[up], base)
            half = jnp.where(below, halves[up], half)
        owner = jnp.right_shift(at * ((1 << 21) // rows + 1), 21)
        inside = at - owner * rows
        group = jnp.right_shift(inside, 4)
        packed = base + (owner & 1) * half + jnp.right_shift(owner, 1) * part + (inside & 15)
        packed = jnp.transpose(group * SPAN + packed)
        for i in range(bnd.shape[0]):
            qb[i * LANES : (i + 1) * LANES, :] = jnp.broadcast_to(
                packed[:, i : i + 1], (LANES, LANES)
            )

    def split_coupling():
        loads[LEVELS].wait()
        for level in range(1, LEVELS):
            at = slice(u_at[level], u_at[level + 1])
            hi, lo = split(uv[:, :, at].reshape(2 * rows, orders[level]))
            uc[: 2 * rows, at] = hi
            uc[2 * rows :, at] = lo

    def select_tiles(level, begin, end):
        span = slice(u_at[level], u_at[level + 1])
        tiles = k_at[level] // TILE

        def one(t, carry):
            g = t // tiles
            k = pl.multiple_of((t - g * tiles) * TILE, TILE)
            want = lane(1) + (g * SPAN + k)
            q = qb[span, :]
            picks = [
                jnp.where(q == want + i * LANES, 1.0, 0.0).astype(BF16)
                for i in range(TILE // LANES)
            ]
            moved = jnp.dot(
                uc[:, span], jnp.concatenate(picks, axis=1), preferred_element_type=F32
            )
            hi, lo = split(moved[: 2 * rows] + moved[2 * rows :])
            ups[level][0, g, :, pl.ds(k, TILE)] = hi
            ups[level][1, g, :, pl.ds(k, TILE)] = lo
            return carry

        lax.fori_loop(begin, end, one, 0, unroll=3)

    def select(wait):
        for tiles in PLAN[wait]:
            select_tiles(*tiles)

    def keep(level, x):
        sol[level * rows : (level + 1) * rows, :] = repeat(x, width)

    first.wait()
    for level in range(LEVELS):
        rt[level, :, :width] = jnp.transpose(rs[:, level].reshape(width, rows))
    select(0)
    pl.semaphore_wait(barrier, chips)
    send(0, 0, rt[0])

    chunk = perm.shape[0]
    col = lax.broadcasted_iota(jnp.int32, (1, chunk), 1)
    block_at = jnp.right_shift(col, 7)
    second = (block_at >= GROUPS).astype(jnp.int32)
    source = (
        jnp.right_shift(col & 127, 4) * (2 * rows)
        + second * rows
        + (block_at - GROUPS * second) * part
        + (col & 15)
    )
    row = lax.broadcasted_iota(jnp.int32, (chunk, chunk), 0)
    perm[...] = jnp.where(row == source, 1.0, 0.0).astype(BF16)
    prepare_diag(0)
    place_boundary()
    split_coupling()
    select(1)
    x = diag_product(0, 0)
    keep(0, x)
    send(1, 0, x)
    select(2)
    prepare_diag(1)
    for level in range(1, LEVELS):
        z = rt[level] - coupling_product(2 * level - 1, level)
        send(2 * level, level, z)
        if level + 1 < LEVELS:
            prepare_diag(level + 1)
            select(2 * level + 1)
        x = diag_product(2 * level, level)
        keep(level, x)
        if level + 1 < LEVELS:
            send(2 * level + 1, level, x)
            select(2 * level + 2)
            multiply_ahead(level + 1)

    loads[-1].wait()
    at = lane(1)

    def pick(j, carry):
        r = [sol[pl.ds(pm[0, GROUPS * j + p], 1), :] for p in range(GROUPS)]
        snd[j] = jnp.where(at < width, r[0], jnp.where(at < 2 * width, r[1], r[2]))
        return carry

    lax.fori_loop(0, chips, pick, 0, unroll=8)
    rcv[leaf] = snd[leaf]
    sizes, steps = offsets(chips)
    for step in steps:
        to = chip(step, sizes, chips)
        pltpu.make_async_remote_copy(
            src_ref=snd.at[to],
            dst_ref=rcv.at[leaf],
            send_sem=send_sem.at[7],
            recv_sem=recv_sem.at[7],
            device_id=(to, sub),
            device_id_type=MESH,
        ).start()
    some = rcv.at[pl.ds(0, chips - 1)]
    pltpu.make_async_copy(some, some, recv_sem.at[7]).wait()
    got = rcv[...].reshape(chips, LANES)
    frm = lax.broadcasted_iota(jnp.int32, (chips, GROUPS * chips), 0)
    to = lax.broadcasted_iota(jnp.int32, (chips, GROUPS * chips), 1)
    total = jnp.zeros((width, GROUPS * chips), F32)
    for p in range(GROUPS):
        place = jnp.where(frm * GROUPS + p == to, 1.0, 0.0)
        moved = lax.dot_general(
            got, place, (((0,), (0,)), ((), ())),
            precision=lax.Precision.HIGHEST, preferred_element_type=F32,
        )
        total = total + moved[p * width : (p + 1) * width]
    out[...] = total

    for stage in range(7):
        level = (stage + 1) // 2 if stage % 2 == 0 else stage // 2
        some = bufs[stage].at[sub, pl.ds(0, (chips >> level) - 1), pl.ds(0, SENT)]
        pltpu.make_async_copy(some, some, send_sem.at[stage]).wait()
        some = bufs[stage].at[sub, :, pl.ds(0, SENT)]
        pltpu.make_async_copy(some, some, send_sem.at[8 + stage]).wait()
    some = snd.at[pl.ds(0, chips - 1)]
    pltpu.make_async_copy(some, some, send_sem.at[7]).wait()


def local(right_sides, diag_inverse, coupling, boundary, plane_map):
    chips = lax.axis_size("leaf")
    rows = right_sides.shape[3]
    part = rows // GROUPS
    width = right_sides.shape[0] * right_sides.shape[2]
    orders = [2 * chips * rows >> level for level in range(LEVELS)]
    d_cols, u_cols = sum(orders), sum(orders[1:])
    chunk = 2 * GROUPS * LANES
    stage_levels = [0, 0, 1, 1, 2, 2, 3]
    packed = [sum(orders[:level]) // GROUPS for level in range(LEVELS)]
    scratch = [
        pltpu.VMEM(right_sides.shape, F32),
        pltpu.VMEM((u_cols // LANES, 1, LANES), jnp.int32),
        pltpu.SMEM(plane_map.shape, jnp.int32),
        pltpu.VMEM((2, rows, d_cols), F32),
        pltpu.VMEM((2, rows, u_cols), F32),
        pltpu.VMEM((2, GROUPS, 2 * rows, d_cols // GROUPS), BF16),
        pltpu.VMEM((4 * rows, u_cols), BF16),
        pltpu.VMEM((chunk, chunk), BF16),
        pltpu.VMEM((u_cols, LANES), jnp.int32),
        pltpu.VMEM((packed[-1], 2 * LANES), BF16),
        pltpu.VMEM((GROUPS * 2 * rows, LANES), F32),
        *[pltpu.VMEM((2, GROUPS, 2 * rows, k), BF16) for k in packed[1:]],
        *[pltpu.VMEM((2, chips >> level, part, LANES), F32) for level in stage_levels],
        pltpu.VMEM((LEVELS, rows, LANES), F32),
        pltpu.VMEM((LEVELS * rows, LANES), F32),
        pltpu.VMEM((chips, 1, LANES), F32),
        pltpu.VMEM((chips, 1, LANES), F32),
        pltpu.SemaphoreType.DMA((LEVELS + 4,)),
        pltpu.SemaphoreType.DMA((16,)),
        pltpu.SemaphoreType.DMA((16,)),
    ]
    vmem, hbm = (pl.BlockSpec(memory_space=s) for s in (pltpu.VMEM, pltpu.HBM))
    field = pl.pallas_call(
        functools.partial(body, chips, rows, orders),
        out_shape=jax.ShapeDtypeStruct((width, GROUPS * chips), F32),
        in_specs=[hbm] * 5,
        out_specs=vmem,
        scratch_shapes=scratch,
        compiler_params=pltpu.CompilerParams(
            collective_id=0, has_side_effects=True, vmem_limit_bytes=60 << 20
        ),
    )(right_sides, diag_inverse, coupling, boundary, plane_map)
    return field.reshape(2, width // 2, GROUPS * chips)


def solution(mesh):
    in_specs = (
        P(None, None, None, ("leaf", "sub")),
        P(None, ("leaf", "sub"), None),
        P(None, ("leaf", "sub"), None),
        P(("leaf", "sub"), None),
        P(("leaf", "sub"), None),
    )
    out_specs = P(None, None, ("leaf", "sub"))
    return jax.shard_map(local, mesh=mesh, in_specs=in_specs, out_specs=out_specs, check_vma=False)
```

```python
import functools

import jax
import jax.numpy as jnp
from jax import lax
from jax.experimental import pallas as pl
from jax.experimental.pallas import tpu as pltpu
from jax.sharding import PartitionSpec as P

LEVELS = 4
SENT = 12
GROUPS = 3
LANES = 128
TILE = 512
SPAN = 4096
DIRECT = 2
PLAN = (
    (),
    ((1, 0, 3),),
    ((1, 3, 12),),
    ((2, 0, 9),),
    ((2, 9, 18),),
    ((3, 0, 9),),
    ((3, 9, 21),),
)
MESH = pl.DeviceIdType.MESH
F32, BF16 = jnp.float32, jnp.bfloat16


def lane(rows):
    return lax.broadcasted_iota(jnp.int32, (rows, LANES), 1)


def roll(x, by):
    return pltpu.roll(x, by % LANES, 1)


def split(x):
    hi = x.astype(BF16)
    return hi, (x - hi.astype(F32)).astype(BF16)


def product(hi, lo, values):
    both = jnp.dot(hi, values, preferred_element_type=F32)
    rest = jnp.dot(lo, values[:, :LANES], preferred_element_type=F32)
    return both[:, :LANES] + both[:, LANES:] + rest


def fold(t, rows, width):
    half = width // 2
    m = 2 * rows
    y = t[:m] + roll(t[m : 2 * m], -width) + roll(t[2 * m :], -2 * width)
    a, b = y[:rows], y[rows:]
    at = lane(rows)
    swapped = jnp.where(at < half, -roll(b, -half), roll(b, half))
    return a + swapped


def pack(x, part, width):
    at = lane(part)
    return jnp.where(
        at < width,
        x[:part],
        jnp.where(
            at < 2 * width, roll(x[part : 2 * part], width), roll(x[2 * part :], 2 * width)
        ),
    )


def squeeze(block, x, part, width):
    last = [x[g * part + 8 : g * part + 16] for g in range(GROUPS)]
    sub8 = lax.broadcasted_iota(jnp.int32, (8, LANES), 0)
    spare = jnp.where(sub8 < 4, pltpu.roll(last[0], 4, 0), last[1])
    free = lane(8) < GROUPS * width
    top = jnp.where(free, block[:8], roll(spare, GROUPS * width))
    low = jnp.where(free, block[8:], roll(pltpu.roll(last[2], 4, 0), GROUPS * width))
    return top, low


def restore(top, low, width):
    at = lax.broadcasted_iota(jnp.int32, top.shape, 2)
    sub8 = lax.broadcasted_iota(jnp.int32, top.shape, 1)
    turn = lambda v, by: pltpu.roll(v, by % LANES, 2)
    outer = jnp.where(at < width, turn(top, width), turn(low, 3 * width))
    outer = pltpu.roll(outer, 4, 1)
    inner = (at >= width) & (at < 2 * width)
    moved = jnp.where(inner, turn(top, 2 * width), outer)
    low = jnp.where(sub8 < 4, low, moved)
    return jnp.concatenate([top, low], axis=1).reshape(-1, LANES)


def repeat(x, width):
    v = jnp.where(lane(x.shape[0]) < width, x, 0.0)
    v = v + roll(v, width)
    return v + roll(v, 2 * width)


def offsets(count):
    sizes = (max(count // 16, 1), min(max(count // 4, 1), 4), min(count, 4))
    steps = [
        (a, b, c)
        for a in range(sizes[0])
        for b in range(sizes[1])
        for c in range(sizes[2])
        if a or b or c
    ]
    hops = lambda step: sum(min(s, n - s) for s, n in zip(step, sizes))
    return sizes, sorted(steps, key=lambda step: -hops(step))


def body(
    chips, rows, orders, rs_hbm, d_hbm, u_hbm, bnd_hbm, pm_hbm, out, *rest
):
    (rs, bnd, pm, dv, uv, dp, uc, perm, qb, xb, ahead), rest = rest[:11], rest[11:]
    ups, bufs, rest = (None,) + rest[:3], rest[3:10], rest[10:]
    place, rt, sol, snd, rcv, load_sem, send_sem, recv_sem = rest
    leaf, sub = lax.axis_index("leaf"), lax.axis_index("sub")
    part = rows // GROUPS
    width = rs_hbm.shape[0] * rs_hbm.shape[2]
    tall = GROUPS * 2 * rows
    d_at = [sum(orders[:a]) for a in range(LEVELS + 1)]
    u_at = [0] + [sum(orders[1:a]) for a in range(1, LEVELS + 1)]
    k_at = [a // GROUPS for a in d_at]
    halves = [n // (2 * GROUPS) for n in orders]

    barrier = pltpu.get_barrier_semaphore()

    def targets(count):
        sizes, steps = offsets(count)
        mine = leaf & (count - 1)
        at = (mine >> 4, (mine >> 2) & 3, mine & 3)
        axes = [
            [((at[i] + s) & (n - 1)) * unit for s in range(n)]
            for i, (n, unit) in enumerate(zip(sizes, (16, 4, 1)))
        ]
        axes[0] = [leaf - mine + z for z in axes[0]]
        planes = [[z + x for x in axes[1]] for z in axes[0]]
        return [(s, planes[s[0]][s[1]] + axes[2][s[2]]) for s in steps]

    everyone = targets(chips)
    for _, to in everyone:
        pl.semaphore_signal(barrier, inc=1, device_id=(to, sub), device_id_type=MESH)
    pl.semaphore_signal(barrier, inc=1, device_id=(leaf, 1 - sub), device_id_type=MESH)

    first = pltpu.make_async_copy(rs_hbm, rs, load_sem.at[LEVELS + 1])
    first.start()
    loads = []
    for level in range(LEVELS):
        span = pl.ds(d_at[level], orders[level])
        loads.append(
            pltpu.make_async_copy(d_hbm.at[:, :, span], dv.at[:, :, span], load_sem.at[level])
        )
    loads.append(pltpu.make_async_copy(u_hbm, uv, load_sem.at[LEVELS]))
    for i in range(bnd.shape[0]):
        pltpu.make_async_copy(
            bnd_hbm.at[:, pl.ds(i * LANES, LANES)], bnd.at[i], load_sem.at[LEVELS + 2]
        ).start()
    loads.append(pltpu.make_async_copy(bnd, bnd, load_sem.at[LEVELS + 2]))
    loads.append(pltpu.make_async_copy(pm_hbm, pm, load_sem.at[LEVELS + 3]))
    for load in (loads[LEVELS], *loads[:LEVELS], loads[-1]):
        load.start()

    def block(level):
        count = chips >> level
        return count, lax.rem(leaf, count)

    def send(stage, level, x):
        buf = bufs[stage]
        count, mine = block(level)
        top, low = squeeze(pack(x, part, width), x, part, width)
        buf[sub, mine, :8] = top
        buf[sub, mine, 8:] = low
        def copy(to, core, sem):
            pltpu.make_async_remote_copy(
                src_ref=buf.at[sub, mine, pl.ds(0, SENT)],
                dst_ref=buf.at[sub, mine, pl.ds(0, SENT)],
                send_sem=send_sem.at[sem],
                recv_sem=recv_sem.at[sem],
                device_id=(to, core),
                device_id_type=MESH,
            ).start()

        for step, to in targets(count) if level else everyone:
            copy(to, sub, stage)
            if level >= DIRECT:
                copy(to, 1 - sub, 8 + stage)
        if level >= DIRECT:
            copy(leaf, 1 - sub, 8 + stage)

    def near(stage, level):
        buf = bufs[stage]
        count, _ = block(level)

        def arrive(blocks, sem):
            some = buf.at[sub, pl.ds(0, blocks), pl.ds(0, SENT)]
            pltpu.make_async_copy(some, some, recv_sem.at[sem]).wait()

        def hand():
            some = buf.at[sub, :, pl.ds(0, SENT)]
            pltpu.make_async_remote_copy(
                src_ref=some,
                dst_ref=some,
                send_sem=send_sem.at[8 + stage],
                recv_sem=recv_sem.at[8 + stage],
                device_id=(leaf, 1 - sub),
                device_id_type=MESH,
            ).start()

        arrive(count - 1, stage)
        if level < DIRECT:
            hand()

    def far(stage, level):
        other = bufs[stage].at[1 - sub, :, pl.ds(0, SENT)]
        pltpu.make_async_copy(other, other, recv_sem.at[8 + stage]).wait()

    def values(stage, level, p):
        buf = bufs[stage]
        rows_of = restore(buf[p, :, :8], buf[p, :, 8:], width)
        return jnp.concatenate(split(rows_of), axis=1)

    def prepare_diag(level):
        loads[level].wait()
        chunk = perm.shape[0]
        for t in range(orders[level] // chunk):
            at = d_at[level] + t * chunk
            hi, lo = split(dv[:, :, at : at + chunk].reshape(2 * rows, chunk))
            both = jnp.concatenate([hi, lo], axis=0)
            moved = jnp.dot(both, perm[...], preferred_element_type=F32).astype(BF16)
            for p in range(2):
                for g in range(GROUPS):
                    to = k_at[level] + p * halves[level] + t * LANES
                    frm = (p * GROUPS + g) * LANES
                    for h in range(2):
                        dp[h, g, :, to : to + LANES] = moved[
                            h * 2 * rows : (h + 1) * 2 * rows, frm : frm + LANES
                        ]

    def both_halves(stage, level, part_of):
        near(stage, level)
        total = part_of(sub)
        far(stage, level)
        return total + part_of(1 - sub)

    def diag_product(stage, level):
        def part_of(p):
            at = pl.ds(pl.multiple_of(k_at[level] + p * halves[level], LANES), halves[level])
            return product(
                dp[0, :, :, at].reshape(tall, halves[level]),
                dp[1, :, :, at].reshape(tall, halves[level]),
                values(stage, level, p),
            )

        return fold(both_halves(stage, level, part_of), rows, width)

    def coupled(level, at, size):
        return product(
            ups[level][0, :, :, pl.ds(at, size)].reshape(tall, size),
            ups[level][1, :, :, pl.ds(at, size)].reshape(tall, size),
            xb[pl.ds(at, size), :],
        )

    def coupling_product(stage, level):
        up = level - 1

        def part_of(p):
            at = pl.multiple_of(k_at[up] + p * halves[up], LANES)
            xb[pl.ds(at, halves[up]), :] = values(stage, up, p)
            return coupled(level, at, halves[up])

        total = both_halves(stage, up, part_of)
        if level > 1:
            total = total + ahead[...]
        return fold(total, rows, width)

    def multiply_ahead(level):
        total = coupled(level, 0, k_at[1])
        for up in range(1, level - 1):
            total = total + coupled(level, k_at[up], k_at[up + 1] - k_at[up])
        ahead[...] = total

    def place_boundary():
        loads[LEVELS + 1].wait()
        index = bnd[...].reshape(bnd.shape[0], LANES)
        at, base, half = index, jnp.zeros_like(index), jnp.full_like(index, halves[0])
        for up in range(1, LEVELS - 1):
            below = index >= d_at[up]
            at = jnp.where(below, index - d_at[up], at)
            base = jnp.where(below, k_at[up], base)
            half = jnp.where(below, halves[up], half)
        owner = jnp.right_shift(at * ((1 << 21) // rows + 1), 21)
        inside = at - owner * rows
        group = jnp.right_shift(inside, 4)
        packed = base + (owner & 1) * half + jnp.right_shift(owner, 1) * part + (inside & 15)
        packed = jnp.transpose(group * SPAN + packed)
        for i in range(bnd.shape[0]):
            qb[i * LANES : (i + 1) * LANES, :] = jnp.broadcast_to(
                packed[:, i : i + 1], (LANES, LANES)
            )

    def split_coupling():
        loads[LEVELS].wait()
        for level in range(1, LEVELS):
            at = slice(u_at[level], u_at[level + 1])
            hi, lo = split(uv[:, :, at].reshape(2 * rows, orders[level]))
            uc[: 2 * rows, at] = hi
            uc[2 * rows :, at] = lo

    def select_tiles(level, begin, end):
        span = slice(u_at[level], u_at[level + 1])
        tiles = k_at[level] // TILE

        def one(t, carry):
            g = t // tiles
            k = pl.multiple_of((t - g * tiles) * TILE, TILE)
            want = lane(1) + (g * SPAN + k)
            q = qb[span, :]
            picks = [
                jnp.where(q == want + i * LANES, 1.0, 0.0).astype(BF16)
                for i in range(TILE // LANES)
            ]
            moved = jnp.dot(
                uc[:, span], jnp.concatenate(picks, axis=1), preferred_element_type=F32
            )
            hi, lo = split(moved[: 2 * rows] + moved[2 * rows :])
            ups[level][0, g, :, pl.ds(k, TILE)] = hi
            ups[level][1, g, :, pl.ds(k, TILE)] = lo
            return carry

        lax.fori_loop(begin, end, one, 0, unroll=3)

    def select(wait):
        for tiles in PLAN[wait]:
            select_tiles(*tiles)

    def keep(level, x):
        sol[level * rows : (level + 1) * rows, :] = repeat(x, width)

    first.wait()
    for level in range(LEVELS):
        rt[level, :, :width] = jnp.transpose(rs[:, level].reshape(width, rows))
    select(0)
    pl.semaphore_wait(barrier, chips)
    send(0, 0, rt[0])

    chunk = perm.shape[0]
    col = lax.broadcasted_iota(jnp.int32, (1, chunk), 1)
    block_at = jnp.right_shift(col, 7)
    second = (block_at >= GROUPS).astype(jnp.int32)
    source = (
        jnp.right_shift(col & 127, 4) * (2 * rows)
        + second * rows
        + (block_at - GROUPS * second) * part
        + (col & 15)
    )
    row = lax.broadcasted_iota(jnp.int32, (chunk, chunk), 0)
    perm[...] = jnp.where(row == source, 1.0, 0.0).astype(BF16)
    prepare_diag(0)
    place_boundary()
    split_coupling()
    select(1)
    x = diag_product(0, 0)
    keep(0, x)
    send(1, 0, x)
    select(2)
    prepare_diag(1)
    frm = lax.broadcasted_iota(jnp.int32, (chips, GROUPS * chips), 0)
    to = lax.broadcasted_iota(jnp.int32, (chips, GROUPS * chips), 1)
    for p in range(GROUPS):
        place[p] = jnp.where(frm * GROUPS + p == to, 1.0, 0.0).astype(BF16)
    for level in range(1, LEVELS):
        z = rt[level] - coupling_product(2 * level - 1, level)
        send(2 * level, level, z)
        if level + 1 < LEVELS:
            prepare_diag(level + 1)
            select(2 * level + 1)
        x = diag_product(2 * level, level)
        keep(level, x)
        if level + 1 < LEVELS:
            send(2 * level + 1, level, x)
            select(2 * level + 2)
            multiply_ahead(level + 1)

    loads[-1].wait()
    at = lane(1)

    def pick(j, carry):
        r = [sol[pl.ds(pm[0, GROUPS * j + p], 1), :] for p in range(GROUPS)]
        snd[j] = jnp.where(at < width, r[0], jnp.where(at < 2 * width, r[1], r[2]))
        return carry

    lax.fori_loop(0, chips, pick, 0, unroll=8)
    rcv[leaf] = snd[leaf]
    for _, to in everyone:
        pltpu.make_async_remote_copy(
            src_ref=snd.at[to],
            dst_ref=rcv.at[leaf],
            send_sem=send_sem.at[7],
            recv_sem=recv_sem.at[7],
            device_id=(to, sub),
            device_id_type=MESH,
        ).start()
    some = rcv.at[pl.ds(0, chips - 1)]
    pltpu.make_async_copy(some, some, recv_sem.at[7]).wait()
    got = rcv[...].reshape(chips, LANES)
    turned = jnp.transpose(got)
    terms = []
    for _ in range(3):
        terms.append(turned.astype(BF16))
        turned = turned - terms[-1].astype(F32)
    total = jnp.zeros((width, GROUPS * chips), F32)
    for p in range(GROUPS):
        term = jnp.concatenate([t[p * width : (p + 1) * width] for t in terms], axis=0)
        moved = jnp.dot(term, place[p], preferred_element_type=F32)
        total = total + (moved[2 * width :] + moved[width : 2 * width] + moved[:width])
    out[...] = total

    for stage in range(7):
        level = (stage + 1) // 2 if stage % 2 == 0 else stage // 2
        some = bufs[stage].at[sub, pl.ds(0, (chips >> level) - 1), pl.ds(0, SENT)]
        pltpu.make_async_copy(some, some, send_sem.at[stage]).wait()
        some = bufs[stage].at[sub, :, pl.ds(0, SENT)]
        pltpu.make_async_copy(some, some, send_sem.at[8 + stage]).wait()
    some = snd.at[pl.ds(0, chips - 1)]
    pltpu.make_async_copy(some, some, send_sem.at[7]).wait()


def local(right_sides, diag_inverse, coupling, boundary, plane_map):
    chips = lax.axis_size("leaf")
    rows = right_sides.shape[3]
    part = rows // GROUPS
    width = right_sides.shape[0] * right_sides.shape[2]
    orders = [2 * chips * rows >> level for level in range(LEVELS)]
    d_cols, u_cols = sum(orders), sum(orders[1:])
    chunk = 2 * GROUPS * LANES
    stage_levels = [0, 0, 1, 1, 2, 2, 3]
    packed = [sum(orders[:level]) // GROUPS for level in range(LEVELS)]
    scratch = [
        pltpu.VMEM(right_sides.shape, F32),
        pltpu.VMEM((u_cols // LANES, 1, LANES), jnp.int32),
        pltpu.SMEM(plane_map.shape, jnp.int32),
        pltpu.VMEM((2, rows, d_cols), F32),
        pltpu.VMEM((2, rows, u_cols), F32),
        pltpu.VMEM((2, GROUPS, 2 * rows, d_cols // GROUPS), BF16),
        pltpu.VMEM((4 * rows, u_cols), BF16),
        pltpu.VMEM((chunk, chunk), BF16),
        pltpu.VMEM((u_cols, LANES), jnp.int32),
        pltpu.VMEM((packed[-1], 2 * LANES), BF16),
        pltpu.VMEM((GROUPS * 2 * rows, LANES), F32),
        *[pltpu.VMEM((2, GROUPS, 2 * rows, k), BF16) for k in packed[1:]],
        *[pltpu.VMEM((2, chips >> level, part, LANES), F32) for level in stage_levels],
        pltpu.VMEM((GROUPS, chips, GROUPS * chips), BF16),
        pltpu.VMEM((LEVELS, rows, LANES), F32),
        pltpu.VMEM((LEVELS * rows, LANES), F32),
        pltpu.VMEM((chips, 1, LANES), F32),
        pltpu.VMEM((chips, 1, LANES), F32),
        pltpu.SemaphoreType.DMA((LEVELS + 4,)),
        pltpu.SemaphoreType.DMA((16,)),
        pltpu.SemaphoreType.DMA((16,)),
    ]
    vmem, hbm = (pl.BlockSpec(memory_space=s) for s in (pltpu.VMEM, pltpu.HBM))
    field = pl.pallas_call(
        functools.partial(body, chips, rows, orders),
        out_shape=jax.ShapeDtypeStruct((width, GROUPS * chips), F32),
        in_specs=[hbm] * 5,
        out_specs=vmem,
        scratch_shapes=scratch,
        compiler_params=pltpu.CompilerParams(
            collective_id=0, has_side_effects=True, vmem_limit_bytes=60 << 20
        ),
    )(right_sides, diag_inverse, coupling, boundary, plane_map)
    return field.reshape(2, width // 2, GROUPS * chips)


def solution(mesh):
    in_specs = (
        P(None, None, None, ("leaf", "sub")),
        P(None, ("leaf", "sub"), None),
        P(None, ("leaf", "sub"), None),
        P(("leaf", "sub"), None),
        P(("leaf", "sub"), None),
    )
    out_specs = P(None, None, ("leaf", "sub"))
    return jax.shard_map(local, mesh=mesh, in_specs=in_specs, out_specs=out_specs, check_vma=False)
```
